256 devices in a mesh: tile: 32 (over z, x), col: 8 (over y, core).
Axes of the slice: x: 4, y: 4, z: 8, core: 2. Of those that a mesh axis runs over, the one named last changes fastest.
Arguments:
- section_image: bfloat16 [12288, 8192], P('tile', 'col'), may hold values from -6 to 6
- peak_offsets: int32 [2, 64, 64], P(None, None, 'col'), may hold values from -8 to 8
Outputs:
- mesh_shift: float32 [2, 96, 64], P(None, 'tile', 'col')
The draws below stay inside these ranges and needn't reach their ends.
All inputs are finite; a program needn't handle non-finite values.
Results may differ from the reference program's by a relative error of at most 0.00075.
Values may be sent and summed in bfloat16 or wider, within the bound.
A program may use at most 64 MiB of HBM per device.

```python
import math
import jax
import jax.numpy as jnp
from jax import lax

SECTIONS = 3
PATCH = 128
PEAK = 8
ITERS = 8
GH = 32
GW = 64


def with_ends(result, stream_key, smallest, high):
    index_at = [jax.random.randint(jax.random.fold_in(stream_key, axis), (), 0, length) for axis, length in enumerate(result.shape)]
    longest = result.shape.index(max(result.shape))
    next_to = index_at[:longest] + [(index_at[longest] + 1) % result.shape[longest]] + index_at[longest + 1:]
    return result.at[tuple(index_at)].set(smallest).at[tuple(next_to)].set(high)


def steps_of(own_key, shape, cuts, least, high):
    loudness, own = 1.0, jax.random.fold_in(own_key, 6)
    for axis_at, blocks in cuts:
        steps = jnp.exp(jax.random.uniform(jax.random.fold_in(own, axis_at), (blocks,), jnp.float32, least / len(cuts), high / len(cuts)))
        loudness = loudness * jnp.repeat(steps, shape[axis_at] // blocks).reshape([-1 if axis == axis_at else 1 for axis in range(len(shape))])
    return loudness


def noise(stream_key, dims, scale, limit, shards=(), held_as=jnp.bfloat16):
    result = scale * jax.random.normal(stream_key, dims, jnp.float32)
    if shards:
        result = result * steps_of(stream_key, dims, shards, -0.22, 0.18)
    return jnp.clip(result, -limit, limit).astype(held_as)


def setup_inputs(seed: int = 0) -> dict:
    seeds = jax.random.split(jax.random.key(seed), 3)
    return {
        "section_image": noise(seeds[0], (SECTIONS * GH * PATCH, GW * PATCH), 1.0, 6.0, ((0, 32), (1, 8))),
        "peak_offsets": with_ends(jax.random.randint(seeds[1], (2, (SECTIONS - 1) * GH, GW), 0 - PEAK, PEAK + 1), jax.random.fold_in(seeds[1], 1), 0 - PEAK, PEAK).astype(jnp.int32),
    }


def dft_tables(length):
    counter = jnp.arange(length, dtype=jnp.int32)
    product = jnp.mod(counter[:, None] * counter[None, :], length)
    phase = product.astype(jnp.float32) * (2.0 * math.pi / length)
    return jnp.cos(phase).astype(jnp.bfloat16), jnp.sin(phase).astype(jnp.bfloat16)


def spectrum(blocks, cosine, sine):
    blk = blocks.astype(jnp.float32)
    cos_f = cosine.astype(jnp.float32)
    sin_f = sine.astype(jnp.float32)
    row_cos = jnp.einsum('ky,nymx->nkmx', cos_f, blk).astype(jnp.bfloat16).astype(jnp.float32)
    row_sin = jnp.einsum('ky,nymx->nkmx', sin_f, blk).astype(jnp.bfloat16).astype(jnp.float32)
    spec_real = (jnp.einsum('nkmx,xl->nkml', row_cos, cos_f) - jnp.einsum('nkmx,xl->nkml', row_sin, sin_f)).astype(jnp.bfloat16)
    spec_imag = (jnp.einsum('nkmx,xl->nkml', row_cos, sin_f) + jnp.einsum('nkmx,xl->nkml', row_sin, cos_f)).astype(jnp.bfloat16)
    return spec_real, spec_imag


def correlate(left_real, left_imag, right_real, right_imag, cosine, sine):
    lr = left_real.astype(jnp.float32)
    li = left_imag.astype(jnp.float32)
    rr = right_real.astype(jnp.float32)
    ri = right_imag.astype(jnp.float32)
    cross_real = (lr * rr + li * ri).astype(jnp.bfloat16).astype(jnp.float32)
    cross_imag = (li * rr - lr * ri).astype(jnp.bfloat16).astype(jnp.float32)
    cos_f = cosine.astype(jnp.float32)
    sin_f = sine.astype(jnp.float32)
    mixed_real = (jnp.einsum('pk,nkml->npml', cos_f, cross_real) - jnp.einsum('pk,nkml->npml', sin_f, cross_imag)).astype(jnp.bfloat16).astype(jnp.float32)
    mixed_imag = (jnp.einsum('pk,nkml->npml', sin_f, cross_real) + jnp.einsum('pk,nkml->npml', cos_f, cross_imag)).astype(jnp.bfloat16).astype(jnp.float32)
    length = cosine.shape[0]
    scale_back = 1.0 / float(length * length * length)
    return (jnp.einsum('npml,lq->npmq', mixed_real, cos_f) - jnp.einsum('npml,lq->npmq', mixed_imag, sin_f)) * scale_back


def flow_of(correlation, peak_row, peak_col):
    count, length, width, _ = correlation.shape
    offsets = jnp.arange(3, dtype=jnp.int32) - 1
    row_pick = jnp.mod(peak_row[:, None, :, None] + offsets[None, :, None, None], length)
    row_pick = jnp.broadcast_to(row_pick, (count, 3, width, length))
    picked = jnp.take_along_axis(correlation, row_pick, axis=1)
    col_pick = jnp.mod(peak_col[:, None, :, None] + offsets[None, None, None, :], length)
    col_pick = jnp.broadcast_to(col_pick, (count, 3, width, 3))
    window = jnp.take_along_axis(picked, col_pick, axis=3)
    window_min = jnp.min(window, axis=(1, 3), keepdims=True)
    weight = window - window_min + 0.5
    weight_sum = jnp.sum(weight, axis=(1, 3))
    steps_f = offsets.astype(jnp.float32)
    flow_row = peak_row.astype(jnp.float32) + jnp.sum(weight * steps_f[None, :, None, None], axis=(1, 3)) / weight_sum
    flow_col = peak_col.astype(jnp.float32) + jnp.sum(weight * steps_f[None, None, None, :], axis=(1, 3)) / weight_sum
    return jnp.stack([flow_row, flow_col])


def reference(section_image, peak_offsets):
    cosine, sine = dft_tables(PATCH)
    pair_rows = (SECTIONS - 1) * GH

    def one_row(pair_row):
        former = lax.dynamic_slice_in_dim(section_image, pair_row * PATCH, PATCH, 0).reshape(1, PATCH, GW, PATCH)
        latter = lax.dynamic_slice_in_dim(section_image, (pair_row + GH) * PATCH, PATCH, 0).reshape(1, PATCH, GW, PATCH)
        former_real, former_imag = spectrum(former, cosine, sine)
        latter_real, latter_imag = spectrum(latter, cosine, sine)
        correlation = correlate(former_real, former_imag, latter_real, latter_imag, cosine, sine)
        row_peaks = lax.dynamic_slice_in_dim(peak_offsets, pair_row, 1, 1)
        return flow_of(correlation, row_peaks[0], row_peaks[1])[:, 0]

    flows = lax.map(one_row, jnp.arange(pair_rows, dtype=jnp.int32))
    flow_field = jnp.concatenate([jnp.transpose(flows, (1, 0, 2)), jnp.zeros((2, GH, GW), jnp.float32)], axis=1)
    all_rows = SECTIONS * GH
    row_number = jnp.arange(all_rows, dtype=jnp.int32)
    row_in_section = jnp.mod(row_number, GH)
    up_ok = (row_in_section != 0)[None, :, None]
    down_ok = (row_in_section != GH - 1)[None, :, None]
    col_number = jnp.arange(GW, dtype=jnp.int32)
    left_ok = (col_number != 0)[None, None, :]
    right_ok = (col_number != GW - 1)[None, None, :]
    pair_ok = (row_number < pair_rows)[None, :, None]
    mesh_shift = jnp.zeros((2, all_rows, GW), jnp.float32)
    for sweep in range(ITERS):
        padded = jnp.pad(mesh_shift, ((0, 0), (1, 1), (1, 1)))
        spring_pull = jnp.where(up_ok, mesh_shift - padded[:, :-2, 1:-1], 0.0)
        spring_pull = spring_pull + jnp.where(down_ok, mesh_shift - padded[:, 2:, 1:-1], 0.0)
        spring_pull = spring_pull + jnp.where(left_ok, mesh_shift - padded[:, 1:-1, :-2], 0.0)
        spring_pull = spring_pull + jnp.where(right_ok, mesh_shift - padded[:, 1:-1, 2:], 0.0)
        ahead_rows = jnp.concatenate([mesh_shift[:, GH:], jnp.zeros((2, GH, GW), jnp.float32)], axis=1)
        pair_error = jnp.where(pair_ok, ahead_rows - mesh_shift - flow_field, 0.0)
        behind_error = jnp.concatenate([jnp.zeros((2, GH, GW), jnp.float32), pair_error[:, :-GH]], axis=1)
        mesh_shift = mesh_shift - 0.12 * (1.0 * spring_pull - pair_error + behind_error)
    return mesh_shift
```

```python
import functools

import jax
import jax.numpy as jnp
from jax import lax
from jax.experimental import pallas as pl
from jax.experimental.pallas import tpu as pltpu
from jax.sharding import PartitionSpec as P

MESH = pl.DeviceIdType.MESH
PATCH = 128
ITERS = 8
TILES = 32
COLS = 8
ROWS = 3
SEC = 32
PAIR_ROWS = 64
HALF = 4
PAD = 16

OWN = tuple(range(-3, 4))
AHEAD = tuple(range(8, 14))
BEHIND = tuple(range(-13, -7))
PEERS = tuple((d, e) for d in OWN + AHEAD + BEHIND for e in (-1, 0, 1) if (d, e) != (0, 0))
SLOT = {peer: i for i, peer in enumerate(PEERS)}
SLOT[(0, 0)] = len(PEERS)

TO_UPPER = ((-11, 0, 1), (-11, 1, 2), (-10, 2, 0))
TO_LOWER = ((11, 1, 0), (11, 2, 1), (10, 0, 2))


def wrap(index, count):
    return lax.rem(index + 2 * count, count)


def kernel(
    peaks, image, out, upper, lower, shifted, sums, message, gathered, field,
    own_sem, send_sem, recv_sem, flow_send, flow_recv,
):
    t = lax.axis_index("tile")
    c = lax.axis_index("col")
    half = HALF * PATCH
    block = ROWS * PATCH

    own_upper = pltpu.make_async_copy(
        image.at[:, pl.ds(0, half)], upper.at[pl.ds(0, block)], own_sem.at[0]
    )
    own_lower = pltpu.make_async_copy(
        image.at[:, pl.ds(half, half)], lower.at[pl.ds(block, block)], own_sem.at[1]
    )
    own_upper.start()
    own_lower.start()

    barrier = pltpu.get_barrier_semaphore()
    for d, e in PEERS:
        pl.semaphore_signal(
            barrier, inc=1, device_id=(wrap(t + d, TILES), wrap(c + e, COLS)), device_id_type=MESH
        )
    pl.semaphore_wait(barrier, len(PEERS))

    def patch_row(buffer, row):
        return buffer.at[pl.ds(row * PATCH, PATCH)]

    sends = []
    for to_upper, to_lower in zip(TO_UPPER, TO_LOWER):
        d, src, dst = to_upper
        sends.append((d, image.at[pl.ds(src * PATCH, PATCH), pl.ds(0, half)], lower, dst))
        d, src, dst = to_lower
        sends.append((d, image.at[pl.ds(src * PATCH, PATCH), pl.ds(half, half)], upper, ROWS + dst))

    def bulk(d, src, buffer, chunk):
        return pltpu.make_async_remote_copy(
            src_ref=src,
            dst_ref=patch_row(buffer, chunk),
            send_sem=send_sem.at[chunk],
            recv_sem=recv_sem.at[chunk],
            device_id=(wrap(t + d, TILES), c),
            device_id_type=MESH,
        )

    def exists(d):
        return t + d >= 0 if d < 0 else t + d < TILES

    for send in sends:

        @pl.when(exists(send[0]))
        def _():
            bulk(*send).start()

    own_upper.wait()
    own_lower.wait()

    def one_pair(chunk, patch, is_lower):
        rows = pl.ds(pl.multiple_of(chunk * PATCH, PATCH), PATCH)
        lanes = pl.ds(patch * PATCH, PATCH)
        pair_row = ROWS * t + chunk - is_lower * (ROWS + SEC)
        py = peaks[0, pair_row, patch + is_lower * HALF]
        px = peaks[1, pair_row, patch + is_lower * HALF]
        later = lower[rows, lanes].astype(jnp.float32)
        later = pltpu.roll(later, lax.rem(PATCH - px, PATCH), 1)
        former = upper[rows, lanes].astype(jnp.float32)
        row = pl.ds(patch * 8 + chunk, 1)
        for b in range(3):
            moved = later if b == 1 else pltpu.roll(later, 1 if b == 0 else PATCH - 1, 1)
            shifted[patch, b, pl.ds(PAD, PATCH)] = moved
            shifted[patch, b, pl.ds(0, PAD)] = moved[PATCH - PAD :]
            shifted[patch, b, pl.ds(PAD + PATCH, PAD)] = moved[:PAD]
        for a in range(3):
            for b in range(3):
                product = former * shifted[patch, b, pl.ds(PAD + py + a - 1, PATCH)]
                sums[3 * a + b, row] = jnp.sum(product, axis=0, keepdims=True)
        sums[9, row] = jnp.full((1, PATCH), py.astype(jnp.float32) * (1.0 / PATCH), jnp.float32)
        sums[10, row] = jnp.full((1, PATCH), px.astype(jnp.float32) * (1.0 / PATCH), jnp.float32)

    def one_chunk(step, carry):
        is_lower = lax.rem(step, 2)
        turn = lax.div(step, 2)
        chunk = jnp.where(is_lower == 1, ROWS + turn, lax.rem(turn + 1, ROWS))
        row = ROWS * t + chunk - is_lower * ROWS
        present = jnp.where(is_lower == 1, row >= SEC, row < PAIR_ROWS)

        @pl.when(present)
        def _():
            buffer = lower
            pltpu.make_async_copy(
                patch_row(buffer, 0), patch_row(buffer, 0), recv_sem.at[chunk]
            ).wait()
            for patch in range(HALF):
                one_pair(chunk, patch, is_lower)

        return carry

    lax.fori_loop(0, 2 * ROWS, one_chunk, 0)

    total = jnp.sum(sums[...], axis=-1, keepdims=True)
    window = [total[i] * (1.0 / PATCH) for i in range(9)]
    least = functools.reduce(jnp.minimum, window)
    weight = [w - least + 0.5 for w in window]
    weight_sum = functools.reduce(jnp.add, weight)
    flow_row = total[9] + (sum(weight[6:9]) - sum(weight[0:3])) / weight_sum
    flow_col = total[10] + (sum(weight[2::3]) - sum(weight[0::3])) / weight_sum
    place = lax.broadcasted_iota(jnp.int32, (8 * HALF, PATCH), 0)
    lane = lax.broadcasted_iota(jnp.int32, (8 * HALF, PATCH), 1)
    chunk = lax.rem(place, 8)
    row = ROWS * t + lax.rem(chunk, ROWS)
    present = ((chunk < ROWS) & (row < PAIR_ROWS)) | (
        (chunk >= ROWS) & (chunk < 2 * ROWS) & (row >= SEC)
    )
    column = COLS * c + lax.div(place, 8) + jnp.where(chunk >= ROWS, HALF, 0)
    spread = jnp.where(
        present & (lane == column),
        flow_row,
        jnp.where(present & (lane == column + PATCH // 2), flow_col, 0.0),
    )
    flows = spread[0:8] + spread[8:16] + spread[16:24] + spread[24:32]
    message[...] = flows
    gathered[SLOT[(0, 0)]] = flows

    copies = [
        pltpu.make_async_remote_copy(
            src_ref=message,
            dst_ref=gathered.at[SLOT[(d, e)]],
            send_sem=flow_send,
            recv_sem=flow_recv,
            device_id=(wrap(t - d, TILES), wrap(c - e, COLS)),
            device_id_type=MESH,
        )
        for d, e in PEERS
    ]
    for copy in copies:
        copy.start()
    field[...] = jnp.zeros_like(field)
    inbox = gathered.at[pl.ds(0, len(PEERS))]
    pltpu.make_async_copy(inbox, inbox, flow_recv).wait()

    for group, (offsets, base) in enumerate(((OWN, 9), (AHEAD, -23), (BEHIND, 41))):
        for d in offsets:
            part = gathered[SLOT[(d, -1)]] + gathered[SLOT[(d, 0)]] + gathered[SLOT[(d, 1)]]
            at = pl.ds(ROWS * d + base, ROWS)
            field[2 * group, at] = part[0:ROWS]
            field[2 * group + 1, at] = part[ROWS : 2 * ROWS]

    size = field.shape[1:]
    flow = [
        field[0] + field[3],
        field[2] + field[5],
        field[4] + field[1],
    ]
    place = lax.broadcasted_iota(jnp.int32, size, 0)
    lane = lax.broadcasted_iota(jnp.int32, size, 1)
    column = lax.rem(lane, PATCH // 2)
    row = lax.rem(ROWS * t - 9 + place + ROWS * TILES, ROWS * TILES)
    in_section = lax.rem(row, SEC)
    up_ok, down_ok = in_section != 0, in_section != SEC - 1
    left_ok, right_ok = column != 0, column != PATCH // 2 - 1
    pair_ok = [lax.rem(row + g * SEC, ROWS * TILES) < PAIR_ROWS for g in range(3)]
    shift = [jnp.zeros(size, jnp.float32) for _ in range(3)]
    for _ in range(ITERS):
        error = [
            jnp.where(pair_ok[g], shift[(g + 1) % 3] - shift[g] - flow[g], 0.0) for g in range(3)
        ]
        after = []
        for g in range(3):
            m = shift[g]
            pull = jnp.where(up_ok, m - pltpu.roll(m, 1, 0), 0.0)
            pull = pull + jnp.where(down_ok, m - pltpu.roll(m, size[0] - 1, 0), 0.0)
            pull = pull + jnp.where(left_ok, m - pltpu.roll(m, 1, 1), 0.0)
            pull = pull + jnp.where(right_ok, m - pltpu.roll(m, PATCH - 1, 1), 0.0)
            after.append(m - 0.12 * (1.0 * pull - error[g] + error[(g + 2) % 3]))
        shift = after
    result = pltpu.roll(shift[0], lax.rem(PATCH - COLS * c, PATCH), 1)
    out[0] = result[9 : 9 + ROWS, 0:COLS]
    out[1] = result[9 : 9 + ROWS, PATCH // 2 : PATCH // 2 + COLS]

    for send in sends:

        @pl.when(exists(send[0]))
        def _():
            bulk(*send).wait_send()

    pltpu.make_async_copy(inbox, inbox, flow_send).wait()


def shards(section_image, peak_offsets):
    half = HALF * PATCH
    return pl.pallas_call(
        kernel,
        out_shape=jax.ShapeDtypeStruct((2, ROWS, COLS), jnp.float32),
        in_specs=[
            pl.BlockSpec(memory_space=pltpu.SMEM),
            pl.BlockSpec(memory_space=pl.ANY),
        ],
        out_specs=pl.BlockSpec(memory_space=pltpu.VMEM),
        scratch_shapes=[
            pltpu.VMEM((2 * ROWS * PATCH, half), jnp.bfloat16),
            pltpu.VMEM((2 * ROWS * PATCH, half), jnp.bfloat16),
            pltpu.VMEM((HALF, 3, PATCH + 2 * PAD, PATCH), jnp.float32),
            pltpu.VMEM((11, 8 * HALF, PATCH), jnp.float32),
            pltpu.VMEM((8, PATCH), jnp.float32),
            pltpu.VMEM((len(PEERS) + 1, 8, PATCH), jnp.float32),
            pltpu.VMEM((6, 24, PATCH), jnp.float32),
            pltpu.SemaphoreType.DMA((2,)),
            pltpu.SemaphoreType.DMA((2 * ROWS,)),
            pltpu.SemaphoreType.DMA((2 * ROWS,)),
            pltpu.SemaphoreType.DMA,
            pltpu.SemaphoreType.DMA,
        ],
        compiler_params=pltpu.CompilerParams(collective_id=0, has_side_effects=True),
        name="flow_and_mesh",
    )(peak_offsets, section_image)


def solution(mesh):
    return jax.shard_map(
        shards,
        mesh=mesh,
        in_specs=(P("tile", "col"), P(None, None, "col")),
        out_specs=P(None, "tile", "col"),
        check_vma=False,
    )
```

```python
import functools

import jax
import jax.numpy as jnp
from jax import lax
from jax.experimental import pallas as pl
from jax.experimental.pallas import tpu as pltpu
from jax.sharding import PartitionSpec as P

MESH = pl.DeviceIdType.MESH
PATCH = 128
ITERS = 8
TILES = 32
COLS = 8
ROWS = 3
SEC = 32
PAIR_ROWS = 64
PAD = 16
DUO = 2

SPLIT = (4,) * PAIR_ROWS
WORDS = tuple(sum(SPLIT[8 * w + i] // DUO << 3 * i for i in range(8)) for w in range(8))

OWN = tuple(range(-3, 4))
AHEAD = tuple(range(8, 14))
BEHIND = tuple(range(-13, -7))
GROUPS = (OWN, AHEAD, BEHIND)
PEERS = tuple((d, e) for g in GROUPS for d in g for e in (-1, 0, 1) if (d, e) != (0, 0))
SLOT = {
    (d, e): (e + 1) * 24 + 8 * g + i
    for g, offsets in enumerate(GROUPS)
    for i, d in enumerate(offsets)
    for e in (-1, 0, 1)
}

TO_UPPER = ((0, -11, 1), (1, -11, 2), (2, -10, 0))
TO_LOWER = ((1, 11, 0), (2, 11, 1), (0, 10, 2))

BULK = ((10, 0), (11, 0), (-10, 0), (-11, 0))
SIDES = ((0, 1), (0, -1))
NEXT = ((1, 0), (-1, 0))
ROUNDS = (BULK + SIDES, BULK + SIDES, BULK + SIDES + NEXT, BULK + NEXT, BULK + NEXT)


def wrap(index, count):
    return lax.rem(index + 2 * count, count)


def kernel(
    peaks, image, out, own, other, offsets, shifted, sums, message, gathered, field,
    own_sem, send_sem, recv_sem, flow_send, flow_recv, told,
):
    t = lax.axis_index("tile")
    c = lax.axis_index("col")
    duos = COLS // DUO
    width = DUO * PATCH

    own_copy = pltpu.make_async_copy(image, own, own_sem.at[0])
    own_copy.start()
    peak_copy = pltpu.make_async_copy(peaks, offsets, own_sem.at[1])
    peak_copy.start()

    def split(pair_row):
        word = jnp.int32(WORDS[0])
        for i in range(1, 8):
            word = jnp.where(lax.div(pair_row, 8) == i, jnp.int32(WORDS[i]), word)
        return lax.shift_right_logical(word, 3 * lax.rem(pair_row, 8)) & 7

    def bounds(is_lower, row):
        pair_row = jnp.clip(row - SEC if is_lower else row, 0, PAIR_ROWS - 1)
        if is_lower:
            return jnp.where(row >= SEC, split(pair_row), duos), duos
        return 0, jnp.where(row < PAIR_ROWS, split(pair_row), 0)

    def exists(d):
        return (t + d >= 0) & (t + d < TILES)

    def tell(semaphore, peers):
        count = jnp.int32(0)
        for d, e in peers:
            count += exists(d).astype(jnp.int32)

            @pl.when(exists(d))
            def _():
                pl.semaphore_signal(
                    semaphore, inc=1, device_id=(t + d, wrap(c + e, COLS)), device_id_type=MESH
                )

        pl.semaphore_wait(semaphore, count)

    tell(pltpu.get_barrier_semaphore(), ROUNDS[0])

    def bulk(kind, row, d, row_there, duo):
        lanes = pl.ds(pl.multiple_of(duo * width, width), width)
        place = kind * ROWS + row_there
        return pltpu.make_async_remote_copy(
            src_ref=image.at[pl.ds(row * PATCH, PATCH), lanes],
            dst_ref=other.at[kind, pl.ds(row_there * PATCH, PATCH), lanes],
            send_sem=send_sem.at[place, duo],
            recv_sem=recv_sem.at[place, duo],
            device_id=(t + d, c),
            device_id_type=MESH,
        )

    def sent(kind, row):
        there = ROWS * t + row + (SEC if kind else -SEC)
        low, high = bounds(kind == 1, there)
        if kind:
            return low, jnp.where(there < SEC * 3, high, low)
        return low, jnp.where(there >= 0, high, low)

    def each_send(act):
        for up, low in zip(TO_UPPER, TO_LOWER):
            for kind, (row, d, row_there) in enumerate((up, low)):

                def step(duo, carry, kind=kind, row=row, d=d, row_there=row_there):
                    act(bulk(kind, row, d, row_there, duo))
                    return carry

                lax.fori_loop(*sent(kind, row), step, 0)

    each_send(lambda copy: copy.start())

    for i, peers in enumerate(ROUNDS[1:]):
        tell(told.at[i], peers)

    own_copy.wait()
    peak_copy.wait()

    def one_pair(kind, row, duo, k):
        patch = duo * DUO + k
        place = kind * ROWS + row
        rows = pl.ds(row * PATCH, PATCH)
        lanes = pl.ds(pl.multiple_of(duo * width, width) + k * PATCH, PATCH)
        pair_row = ROWS * t + row - kind * SEC
        py = offsets[0, patch, pair_row]
        px = offsets[1, patch, pair_row]
        mine = own[rows, lanes].astype(jnp.float32)
        theirs = other[kind, rows, lanes].astype(jnp.float32)
        former, later = (theirs, mine) if kind else (mine, theirs)
        later = pltpu.roll(later, lax.rem(PATCH - px, PATCH), 1)
        for b in range(3):
            moved = later if b == 1 else pltpu.roll(later, 1 if b == 0 else PATCH - 1, 1)
            shifted[k, b, pl.ds(PAD, PATCH)] = moved
            shifted[k, b, pl.ds(0, PAD)] = moved[PATCH - PAD :]
            shifted[k, b, pl.ds(PAD + PATCH, PAD)] = moved[:PAD]
        at = pl.ds(patch * 8 + place, 1)
        for a in range(3):
            for b in range(3):
                product = former * shifted[k, b, pl.ds(PAD + py + a - 1, PATCH)]
                sums[3 * a + b, at] = jnp.sum(product, axis=0, keepdims=True)
        sums[9, at] = jnp.full((1, PATCH), py.astype(jnp.float32) * (1.0 / PATCH), jnp.float32)
        sums[10, at] = jnp.full((1, PATCH), px.astype(jnp.float32) * (1.0 / PATCH), jnp.float32)

    for up, low in zip(TO_UPPER, TO_LOWER):
        for kind, (_, _, row) in enumerate((up, low)):

            def step(duo, carry, kind=kind, row=row):
                lanes = pl.ds(pl.multiple_of(duo * width, width), width)
                part = other.at[kind, pl.ds(row * PATCH, PATCH), lanes]
                pltpu.make_async_copy(part, part, recv_sem.at[kind * ROWS + row, duo]).wait()
                for k in range(DUO):
                    one_pair(kind, row, duo, k)
                return carry

            lax.fori_loop(*bounds(kind == 1, ROWS * t + row), step, 0)

    total = jnp.sum(sums[...], axis=-1, keepdims=True)
    window = [total[i] * (1.0 / PATCH) for i in range(9)]
    least = functools.reduce(jnp.minimum, window)
    weight = [w - least + 0.5 for w in window]
    weight_sum = functools.reduce(jnp.add, weight)
    flow_row = total[9] + (sum(weight[6:9]) - sum(weight[0:3])) / weight_sum
    flow_col = total[10] + (sum(weight[2::3]) - sum(weight[0::3])) / weight_sum
    line = lax.broadcasted_iota(jnp.int32, (8 * COLS, PATCH), 0)
    lane = lax.broadcasted_iota(jnp.int32, (8 * COLS, PATCH), 1)
    place = lax.rem(line, 8)
    patch = lax.div(line, 8)
    present = line < 0
    for kind in range(2):
        for row in range(ROWS):
            low, high = bounds(kind == 1, ROWS * t + row)
            present |= (place == kind * ROWS + row) & (patch >= DUO * low) & (patch < DUO * high)
    column = COLS * lax.rem(c + place, COLS) + patch
    half = PATCH // 2
    flows = jnp.where(
        present & (lane == column),
        flow_row,
        jnp.where(present & (lane == column + half), flow_col, 0.0),
    )
    flows = jnp.sum(flows, axis=0, keepdims=True)
    message[...] = flows
    gathered[pl.ds(SLOT[(0, 0)], 1)] = flows

    copies = [
        pltpu.make_async_remote_copy(
            src_ref=message,
            dst_ref=gathered.at[pl.ds(SLOT[(d, e)], 1)],
            send_sem=flow_send,
            recv_sem=flow_recv,
            device_id=(wrap(t - d, TILES), wrap(c - e, COLS)),
            device_id_type=MESH,
        )
        for d, e in PEERS
    ]
    for copy in copies:
        copy.start()
    field[...] = jnp.zeros_like(field)
    each_send(lambda copy: copy.wait_send())
    inbox = gathered.at[pl.ds(0, len(PEERS))]
    pltpu.make_async_copy(inbox, inbox, flow_recv).wait()

    lane = lax.broadcasted_iota(jnp.int32, (24, PATCH), 1)
    in_half = lax.rem(lane, half)
    group = lax.div(in_half, COLS)
    for q in range(2 * ROWS):
        part = jnp.zeros((24, PATCH), jnp.float32)
        for e in (-1, 0, 1):
            part += jnp.where(
                group == lax.rem(c + e + q + COLS, COLS), gathered[pl.ds((e + 1) * 24, 24)], 0.0
            )
        if q:
            near = pltpu.roll(part, PATCH - COLS * q, 1)
            far = pltpu.roll(part, half - COLS * q, 1)
            part = jnp.where(in_half + COLS * q < half, near, far)
        kind, row = divmod(q, ROWS)
        for g, tiles in enumerate(GROUPS):
            field[kind, g, pl.ds(row + g, len(tiles), stride=ROWS)] = part[8 * g : 8 * g + len(tiles)]

    size = field.shape[2:]
    flow = [field[0, g] + field[1, (g + 1) % 3] for g in range(3)]
    line = lax.broadcasted_iota(jnp.int32, size, 0)
    lane = lax.broadcasted_iota(jnp.int32, size, 1)
    column = lax.rem(lane, half)
    row = lax.rem(ROWS * t - 9 + line + ROWS * TILES, ROWS * TILES)
    in_section = lax.rem(row, SEC)
    up_ok, down_ok = in_section != 0, in_section != SEC - 1
    left_ok, right_ok = column != 0, column != half - 1
    pair_ok = [lax.rem(row + g * SEC, ROWS * TILES) < PAIR_ROWS for g in range(3)]
    shift = [jnp.zeros(size, jnp.float32) for _ in range(3)]
    for _ in range(ITERS):
        error = [
            jnp.where(pair_ok[g], shift[(g + 1) % 3] - shift[g] - flow[g], 0.0) for g in range(3)
        ]
        after = []
        for g in range(3):
            m = shift[g]
            pull = jnp.where(up_ok, m - pltpu.roll(m, 1, 0), 0.0)
            pull = pull + jnp.where(down_ok, m - pltpu.roll(m, size[0] - 1, 0), 0.0)
            pull = pull + jnp.where(left_ok, m - pltpu.roll(m, 1, 1), 0.0)
            pull = pull + jnp.where(right_ok, m - pltpu.roll(m, PATCH - 1, 1), 0.0)
            after.append(m - 0.12 * (1.0 * pull - error[g] + error[(g + 2) % 3]))
        shift = after
    result = pltpu.roll(shift[0], lax.rem(PATCH - COLS * c, PATCH), 1)
    for row in range(ROWS):
        out[row, pl.ds(0, 1)] = result[9 + row : 10 + row, 0:COLS]
        out[row, pl.ds(1, 1)] = result[9 + row : 10 + row, half : half + COLS]

    pltpu.make_async_copy(inbox, inbox, flow_send).wait()


def shards(section_image, peak_offsets):
    block = section_image.shape
    places = (2 * ROWS, COLS // DUO)
    result = pl.pallas_call(
        kernel,
        out_shape=jax.ShapeDtypeStruct((ROWS, 2, COLS), jnp.float32),
        in_specs=[pl.BlockSpec(memory_space=pl.ANY)] * 2,
        out_specs=pl.BlockSpec(memory_space=pltpu.VMEM),
        scratch_shapes=[
            pltpu.VMEM(block, jnp.bfloat16),
            pltpu.VMEM((2, *block), jnp.bfloat16),
            pltpu.SMEM((2, COLS, PAIR_ROWS), jnp.int32),
            pltpu.VMEM((DUO, 3, PATCH + 2 * PAD, PATCH), jnp.float32),
            pltpu.VMEM((11, 8 * COLS, PATCH), jnp.float32),
            pltpu.VMEM((1, PATCH), jnp.float32),
            pltpu.VMEM((72, PATCH), jnp.float32),
            pltpu.VMEM((2, 3, 24, PATCH), jnp.float32),
            pltpu.SemaphoreType.DMA((2,)),
            pltpu.SemaphoreType.DMA(places),
            pltpu.SemaphoreType.DMA(places),
            pltpu.SemaphoreType.DMA,
            pltpu.SemaphoreType.DMA,
            pltpu.SemaphoreType.REGULAR((len(ROUNDS) - 1,)),
        ],
        compiler_params=pltpu.CompilerParams(collective_id=0, has_side_effects=True),
        name="flow_and_mesh",
    )(peak_offsets.transpose(0, 2, 1), section_image)
    return result.transpose(1, 0, 2)


def solution(mesh):
    return jax.shard_map(
        shards,
        mesh=mesh,
        in_specs=(P("tile", "col"), P(None, None, "col")),
        out_specs=P(None, "tile", "col"),
        check_vma=False,
    )
```

```python
import functools

import jax
import jax.numpy as jnp
from jax import lax
from jax.experimental import pallas as pl
from jax.experimental.pallas import tpu as pltpu
from jax.sharding import PartitionSpec as P

MESH = pl.DeviceIdType.MESH
PATCH = 128
ITERS = 8
TILES = 32
COLS = 8
ROWS = 3
SEC = 32
PAIR_ROWS = 64
PAD = 16
DUO = 2

SPLIT = (
    4, 4, 4, 4, 4, 4, 4, 4, 4, 4, 4, 4, 4, 4, 4, 8,
    4, 4, 4, 4, 4, 4, 4, 4, 0, 4, 4, 6, 2, 0, 8, 4,
    4, 2, 8, 6, 0, 4, 4, 8, 4, 4, 4, 4, 4, 4, 4, 4,
    4, 4, 4, 6, 4, 4, 4, 4, 4, 4, 4, 4, 4, 4, 4, 4,
)
WORDS = tuple(sum(SPLIT[8 * w + i] // DUO << 3 * i for i in range(8)) for w in range(8))

OWN = tuple(range(-3, 4))
AHEAD = tuple(range(8, 14))
BEHIND = tuple(range(-13, -7))
GROUPS = (OWN, AHEAD, BEHIND)
PEERS = tuple((d, e) for g in GROUPS for d in g for e in (-1, 0, 1) if (d, e) != (0, 0))
SLOT = {
    (d, e): (e + 1) * 24 + 8 * g + i
    for g, offsets in enumerate(GROUPS)
    for i, d in enumerate(offsets)
    for e in (-1, 0, 1)
}

TO_UPPER = ((2, -10, 0), (0, -11, 1), (1, -11, 2))
TO_LOWER = ((0, 10, 2), (1, 11, 0), (2, 11, 1))

BULK = ((10, 0), (11, 0), (-10, 0), (-11, 0))
SIDES = ((0, 1), (0, -1))
NEXT = ((1, 0), (-1, 0))
ROUNDS = (BULK + SIDES, BULK + SIDES, BULK + SIDES + NEXT, BULK + NEXT, BULK + NEXT)


def wrap(index, count):
    return lax.rem(index + 2 * count, count)


def kernel(
    peaks, image, out, own, other, offsets, shifted, sums, message, gathered, field,
    own_sem, send_sem, recv_sem, flow_send, flow_recv, told,
):
    t = lax.axis_index("tile")
    c = lax.axis_index("col")
    duos = COLS // DUO
    width = DUO * PATCH

    own_copy = pltpu.make_async_copy(image, own, own_sem.at[0])
    own_copy.start()
    peak_copy = pltpu.make_async_copy(peaks, offsets, own_sem.at[1])
    peak_copy.start()

    def split(pair_row):
        word = jnp.int32(WORDS[0])
        for i in range(1, 8):
            word = jnp.where(lax.div(pair_row, 8) == i, jnp.int32(WORDS[i]), word)
        return lax.shift_right_logical(word, 3 * lax.rem(pair_row, 8)) & 7

    def bounds(is_lower, row):
        pair_row = jnp.clip(row - SEC if is_lower else row, 0, PAIR_ROWS - 1)
        if is_lower:
            return jnp.where(row >= SEC, split(pair_row), duos), duos
        return 0, jnp.where(row < PAIR_ROWS, split(pair_row), 0)

    def exists(d):
        return (t + d >= 0) & (t + d < TILES)

    def tell(semaphore, peers):
        count = jnp.int32(0)
        for d, e in peers:
            count += exists(d).astype(jnp.int32)

            @pl.when(exists(d))
            def _():
                pl.semaphore_signal(
                    semaphore, inc=1, device_id=(t + d, wrap(c + e, COLS)), device_id_type=MESH
                )

        pl.semaphore_wait(semaphore, count)

    tell(pltpu.get_barrier_semaphore(), ROUNDS[0])

    def bulk(kind, row, d, row_there, duo):
        lanes = pl.ds(pl.multiple_of(duo * width, width), width)
        place = kind * ROWS + row_there
        return pltpu.make_async_remote_copy(
            src_ref=image.at[pl.ds(row * PATCH, PATCH), lanes],
            dst_ref=other.at[kind, pl.ds(row_there * PATCH, PATCH), lanes],
            send_sem=send_sem.at[place, duo],
            recv_sem=recv_sem.at[place, duo],
            device_id=(t + d, c),
            device_id_type=MESH,
        )

    def sent(kind, row):
        there = ROWS * t + row + (SEC if kind else -SEC)
        low, high = bounds(kind == 1, there)
        if kind:
            return low, jnp.where(there < SEC * 3, high, low)
        return low, jnp.where(there >= 0, high, low)

    def each_send(act):
        for up, low in zip(TO_UPPER, TO_LOWER):
            for kind, (row, d, row_there) in enumerate((up, low)):

                def step(duo, carry, kind=kind, row=row, d=d, row_there=row_there):
                    act(bulk(kind, row, d, row_there, duo))
                    return carry

                lax.fori_loop(*sent(kind, row), step, 0)

    each_send(lambda copy: copy.start())

    for i, peers in enumerate(ROUNDS[1:]):
        tell(told.at[i], peers)

    own_copy.wait()
    peak_copy.wait()

    def one_pair(kind, row, duo, k):
        patch = duo * DUO + k
        place = kind * ROWS + row
        rows = pl.ds(row * PATCH, PATCH)
        lanes = pl.ds(pl.multiple_of(duo * width, width) + k * PATCH, PATCH)
        pair_row = ROWS * t + row - kind * SEC
        py = offsets[0, patch, pair_row]
        px = offsets[1, patch, pair_row]
        mine = own[rows, lanes].astype(jnp.float32)
        theirs = other[kind, rows, lanes].astype(jnp.float32)
        former, later = (theirs, mine) if kind else (mine, theirs)
        later = pltpu.roll(later, lax.rem(PATCH - px, PATCH), 1)
        for b in range(3):
            moved = later if b == 1 else pltpu.roll(later, 1 if b == 0 else PATCH - 1, 1)
            shifted[k, b, pl.ds(PAD, PATCH)] = moved
            shifted[k, b, pl.ds(0, PAD)] = moved[PATCH - PAD :]
            shifted[k, b, pl.ds(PAD + PATCH, PAD)] = moved[:PAD]
        at = pl.ds(patch * 8 + place, 1)
        for a in range(3):
            for b in range(3):
                product = former * shifted[k, b, pl.ds(PAD + py + a - 1, PATCH)]
                sums[3 * a + b, at] = jnp.sum(product, axis=0, keepdims=True)
        sums[9, at] = jnp.full((1, PATCH), py.astype(jnp.float32) * (1.0 / PATCH), jnp.float32)
        sums[10, at] = jnp.full((1, PATCH), px.astype(jnp.float32) * (1.0 / PATCH), jnp.float32)

    for up, low in zip(TO_UPPER, TO_LOWER):
        for kind, (_, _, row) in enumerate((up, low)):

            def step(duo, carry, kind=kind, row=row):
                lanes = pl.ds(pl.multiple_of(duo * width, width), width)
                part = other.at[kind, pl.ds(row * PATCH, PATCH), lanes]
                pltpu.make_async_copy(part, part, recv_sem.at[kind * ROWS + row, duo]).wait()
                for k in range(DUO):
                    one_pair(kind, row, duo, k)
                return carry

            lax.fori_loop(*bounds(kind == 1, ROWS * t + row), step, 0)

    total = jnp.sum(sums[...], axis=-1, keepdims=True)
    window = [total[i] * (1.0 / PATCH) for i in range(9)]
    least = functools.reduce(jnp.minimum, window)
    weight = [w - least + 0.5 for w in window]
    weight_sum = functools.reduce(jnp.add, weight)
    flow_row = total[9] + (sum(weight[6:9]) - sum(weight[0:3])) / weight_sum
    flow_col = total[10] + (sum(weight[2::3]) - sum(weight[0::3])) / weight_sum
    line = lax.broadcasted_iota(jnp.int32, (8 * COLS, PATCH), 0)
    lane = lax.broadcasted_iota(jnp.int32, (8 * COLS, PATCH), 1)
    place = lax.rem(line, 8)
    patch = lax.div(line, 8)
    present = line < 0
    for kind in range(2):
        for row in range(ROWS):
            low, high = bounds(kind == 1, ROWS * t + row)
            present |= (place == kind * ROWS + row) & (patch >= DUO * low) & (patch < DUO * high)
    column = COLS * lax.rem(c + place, COLS) + patch
    half = PATCH // 2
    flows = jnp.where(
        present & (lane == column),
        flow_row,
        jnp.where(present & (lane == column + half), flow_col, 0.0),
    )
    flows = jnp.sum(flows, axis=0, keepdims=True)
    message[...] = flows
    gathered[pl.ds(SLOT[(0, 0)], 1)] = flows

    copies = [
        pltpu.make_async_remote_copy(
            src_ref=message,
            dst_ref=gathered.at[pl.ds(SLOT[(d, e)], 1)],
            send_sem=flow_send,
            recv_sem=flow_recv,
            device_id=(wrap(t - d, TILES), wrap(c - e, COLS)),
            device_id_type=MESH,
        )
        for d, e in PEERS
    ]
    for copy in copies:
        copy.start()
    field[...] = jnp.zeros_like(field)
    each_send(lambda copy: copy.wait_send())
    inbox = gathered.at[pl.ds(0, len(PEERS))]
    pltpu.make_async_copy(inbox, inbox, flow_recv).wait()

    lane = lax.broadcasted_iota(jnp.int32, (24, PATCH), 1)
    in_half = lax.rem(lane, half)
    group = lax.div(in_half, COLS)
    for q in range(2 * ROWS):
        part = jnp.zeros((24, PATCH), jnp.float32)
        for e in (-1, 0, 1):
            part += jnp.where(
                group == lax.rem(c + e + q + COLS, COLS), gathered[pl.ds((e + 1) * 24, 24)], 0.0
            )
        if q:
            near = pltpu.roll(part, PATCH - COLS * q, 1)
            far = pltpu.roll(part, half - COLS * q, 1)
            part = jnp.where(in_half + COLS * q < half, near, far)
        kind, row = divmod(q, ROWS)
        for g, tiles in enumerate(GROUPS):
            field[kind, g, pl.ds(row + g, len(tiles), stride=ROWS)] = part[8 * g : 8 * g + len(tiles)]

    size = field.shape[2:]
    flow = [field[0, g] + field[1, (g + 1) % 3] for g in range(3)]
    line = lax.broadcasted_iota(jnp.int32, size, 0)
    lane = lax.broadcasted_iota(jnp.int32, size, 1)
    column = lax.rem(lane, half)
    row = lax.rem(ROWS * t - 9 + line + ROWS * TILES, ROWS * TILES)
    in_section = lax.rem(row, SEC)
    up_ok, down_ok = in_section != 0, in_section != SEC - 1
    left_ok, right_ok = column != 0, column != half - 1
    pair_ok = [lax.rem(row + g * SEC, ROWS * TILES) < PAIR_ROWS for g in range(3)]
    shift = [jnp.zeros(size, jnp.float32) for _ in range(3)]
    for _ in range(ITERS):
        error = [
            jnp.where(pair_ok[g], shift[(g + 1) % 3] - shift[g] - flow[g], 0.0) for g in range(3)
        ]
        after = []
        for g in range(3):
            m = shift[g]
            pull = jnp.where(up_ok, m - pltpu.roll(m, 1, 0), 0.0)
            pull = pull + jnp.where(down_ok, m - pltpu.roll(m, size[0] - 1, 0), 0.0)
            pull = pull + jnp.where(left_ok, m - pltpu.roll(m, 1, 1), 0.0)
            pull = pull + jnp.where(right_ok, m - pltpu.roll(m, PATCH - 1, 1), 0.0)
            after.append(m - 0.12 * (1.0 * pull - error[g] + error[(g + 2) % 3]))
        shift = after
    result = pltpu.roll(shift[0], lax.rem(PATCH - COLS * c, PATCH), 1)
    for row in range(ROWS):
        out[row, pl.ds(0, 1)] = result[9 + row : 10 + row, 0:COLS]
        out[row, pl.ds(1, 1)] = result[9 + row : 10 + row, half : half + COLS]

    pltpu.make_async_copy(inbox, inbox, flow_send).wait()


def shards(section_image, peak_offsets):
    block = section_image.shape
    places = (2 * ROWS, COLS // DUO)
    result = pl.pallas_call(
        kernel,
        out_shape=jax.ShapeDtypeStruct((ROWS, 2, COLS), jnp.float32),
        in_specs=[pl.BlockSpec(memory_space=pl.ANY)] * 2,
        out_specs=pl.BlockSpec(memory_space=pltpu.VMEM),
        scratch_shapes=[
            pltpu.VMEM(block, jnp.bfloat16),
            pltpu.VMEM((2, *block), jnp.bfloat16),
            pltpu.SMEM((2, COLS, PAIR_ROWS), jnp.int32),
            pltpu.VMEM((DUO, 3, PATCH + 2 * PAD, PATCH), jnp.float32),
            pltpu.VMEM((11, 8 * COLS, PATCH), jnp.float32),
            pltpu.VMEM((1, PATCH), jnp.float32),
            pltpu.VMEM((72, PATCH), jnp.float32),
            pltpu.VMEM((2, 3, 24, PATCH), jnp.float32),
            pltpu.SemaphoreType.DMA((2,)),
            pltpu.SemaphoreType.DMA(places),
            pltpu.SemaphoreType.DMA(places),
            pltpu.SemaphoreType.DMA,
            pltpu.SemaphoreType.DMA,
            pltpu.SemaphoreType.REGULAR((len(ROUNDS) - 1,)),
        ],
        compiler_params=pltpu.CompilerParams(collective_id=0, has_side_effects=True),
        name="flow_and_mesh",
    )(peak_offsets.transpose(0, 2, 1), section_image)
    return result.transpose(1, 0, 2)


def solution(mesh):
    return jax.shard_map(
        shards,
        mesh=mesh,
        in_specs=(P("tile", "col"), P(None, None, "col")),
        out_specs=P(None, "tile", "col"),
        check_vma=False,
    )
```

```python
import functools

import jax
import jax.numpy as jnp
from jax import lax
from jax.experimental import pallas as pl
from jax.experimental.pallas import tpu as pltpu
from jax.sharding import PartitionSpec as P

MESH = pl.DeviceIdType.MESH
PATCH = 128
ITERS = 8
TILES = 32
COLS = 8
ROWS = 3
SEC = 32
PAIR_ROWS = 64
PAD = 16
DUO = 2

SPLIT = (
    4, 4, 4, 4, 4, 4, 4, 4, 4, 4, 6, 4, 4, 4, 4, 8,
    4, 4, 4, 4, 4, 4, 4, 4, 0, 4, 4, 6, 2, 0, 8, 4,
    4, 2, 8, 6, 0, 4, 6, 8, 4, 4, 4, 4, 2, 4, 4, 4,
    4, 4, 2, 4, 4, 4, 4, 2, 4, 4, 4, 4, 4, 4, 2, 4,
)
WORDS = tuple(sum(SPLIT[8 * w + i] // DUO << 3 * i for i in range(8)) for w in range(8))

OWN = tuple(range(-3, 4))
AHEAD = tuple(range(8, 14))
BEHIND = tuple(range(-13, -7))
GROUPS = (OWN, AHEAD, BEHIND)
PEERS = tuple((d, e) for g in GROUPS for d in g for e in (-1, 0, 1) if (d, e) != (0, 0))
SLOT = {
    (d, e): (e + 1) * 24 + 8 * g + i
    for g, offsets in enumerate(GROUPS)
    for i, d in enumerate(offsets)
    for e in (-1, 0, 1)
}

TO_UPPER = ((2, -10, 0), (0, -11, 1), (1, -11, 2))
TO_LOWER = ((0, 10, 2), (1, 11, 0), (2, 11, 1))

BULK = ((10, 0), (11, 0), (-10, 0), (-11, 0))
SIDES = ((0, 1), (0, -1))
NEXT = ((1, 0), (-1, 0))
ROUNDS = (BULK + SIDES, BULK + SIDES, BULK + SIDES + NEXT, BULK + NEXT, BULK + NEXT)


def wrap(index, count):
    return lax.rem(index + 2 * count, count)


def kernel(
    peaks, image, out, own, other, offsets, shifted, sums, message, gathered, field,
    own_sem, send_sem, recv_sem, flow_send, flow_recv, told,
):
    t = lax.axis_index("tile")
    c = lax.axis_index("col")
    duos = COLS // DUO
    width = DUO * PATCH

    own_copy = pltpu.make_async_copy(image, own, own_sem.at[0])
    own_copy.start()
    peak_copy = pltpu.make_async_copy(peaks, offsets, own_sem.at[1])
    peak_copy.start()

    def split(pair_row):
        word = jnp.int32(WORDS[0])
        for i in range(1, 8):
            word = jnp.where(lax.div(pair_row, 8) == i, jnp.int32(WORDS[i]), word)
        return lax.shift_right_logical(word, 3 * lax.rem(pair_row, 8)) & 7

    def bounds(is_lower, row):
        pair_row = jnp.clip(row - SEC if is_lower else row, 0, PAIR_ROWS - 1)
        if is_lower:
            return jnp.where(row >= SEC, split(pair_row), duos), duos
        return 0, jnp.where(row < PAIR_ROWS, split(pair_row), 0)

    def exists(d):
        return (t + d >= 0) & (t + d < TILES)

    def tell(semaphore, peers):
        count = jnp.int32(0)
        for d, e in peers:
            count += exists(d).astype(jnp.int32)

            @pl.when(exists(d))
            def _():
                pl.semaphore_signal(
                    semaphore, inc=1, device_id=(t + d, wrap(c + e, COLS)), device_id_type=MESH
                )

        pl.semaphore_wait(semaphore, count)

    tell(pltpu.get_barrier_semaphore(), ROUNDS[0])

    def bulk(kind, row, d, row_there, duo):
        lanes = pl.ds(pl.multiple_of(duo * width, width), width)
        place = kind * ROWS + row_there
        return pltpu.make_async_remote_copy(
            src_ref=image.at[pl.ds(row * PATCH, PATCH), lanes],
            dst_ref=other.at[kind, pl.ds(row_there * PATCH, PATCH), lanes],
            send_sem=send_sem.at[place, duo],
            recv_sem=recv_sem.at[place, duo],
            device_id=(t + d, c),
            device_id_type=MESH,
        )

    def sent(kind, row):
        there = ROWS * t + row + (SEC if kind else -SEC)
        low, high = bounds(kind == 1, there)
        if kind:
            return low, jnp.where(there < SEC * 3, high, low)
        return low, jnp.where(there >= 0, high, low)

    def each_send(act):
        for up, low in zip(TO_UPPER, TO_LOWER):
            for kind, (row, d, row_there) in enumerate((up, low)):

                def step(duo, carry, kind=kind, row=row, d=d, row_there=row_there):
                    act(bulk(kind, row, d, row_there, duo))
                    return carry

                lax.fori_loop(*sent(kind, row), step, 0)

    each_send(lambda copy: copy.start())

    for i, peers in enumerate(ROUNDS[1:]):
        tell(told.at[i], peers)

    own_copy.wait()
    peak_copy.wait()

    def one_pair(kind, row, duo, k):
        patch = duo * DUO + k
        place = kind * ROWS + row
        rows = pl.ds(row * PATCH, PATCH)
        lanes = pl.ds(pl.multiple_of(duo * width, width) + k * PATCH, PATCH)
        pair_row = ROWS * t + row - kind * SEC
        py = offsets[0, patch, pair_row]
        px = offsets[1, patch, pair_row]
        mine = own[rows, lanes].astype(jnp.float32)
        theirs = other[kind, rows, lanes].astype(jnp.float32)
        former, later = (theirs, mine) if kind else (mine, theirs)
        later = pltpu.roll(later, lax.rem(PATCH - px, PATCH), 1)
        for b in range(3):
            moved = later if b == 1 else pltpu.roll(later, 1 if b == 0 else PATCH - 1, 1)
            shifted[k, b, pl.ds(PAD, PATCH)] = moved
            shifted[k, b, pl.ds(0, PAD)] = moved[PATCH - PAD :]
            shifted[k, b, pl.ds(PAD + PATCH, PAD)] = moved[:PAD]
        at = pl.ds(patch * 8 + place, 1)
        for a in range(3):
            for b in range(3):
                product = former * shifted[k, b, pl.ds(PAD + py + a - 1, PATCH)]
                sums[3 * a + b, at] = jnp.sum(product, axis=0, keepdims=True)
        sums[9, at] = jnp.full((1, PATCH), py.astype(jnp.float32) * (1.0 / PATCH), jnp.float32)
        sums[10, at] = jnp.full((1, PATCH), px.astype(jnp.float32) * (1.0 / PATCH), jnp.float32)

    for up, low in zip(TO_UPPER, TO_LOWER):
        for kind, (_, _, row) in enumerate((up, low)):

            def step(duo, carry, kind=kind, row=row):
                lanes = pl.ds(pl.multiple_of(duo * width, width), width)
                part = other.at[kind, pl.ds(row * PATCH, PATCH), lanes]
                pltpu.make_async_copy(part, part, recv_sem.at[kind * ROWS + row, duo]).wait()
                for k in range(DUO):
                    one_pair(kind, row, duo, k)
                return carry

            lax.fori_loop(*bounds(kind == 1, ROWS * t + row), step, 0)

    total = jnp.sum(sums[...], axis=-1, keepdims=True)
    window = [total[i] * (1.0 / PATCH) for i in range(9)]
    least = functools.reduce(jnp.minimum, window)
    weight = [w - least + 0.5 for w in window]
    weight_sum = functools.reduce(jnp.add, weight)
    flow_row = total[9] + (sum(weight[6:9]) - sum(weight[0:3])) / weight_sum
    flow_col = total[10] + (sum(weight[2::3]) - sum(weight[0::3])) / weight_sum
    line = lax.broadcasted_iota(jnp.int32, (8 * COLS, PATCH), 0)
    lane = lax.broadcasted_iota(jnp.int32, (8 * COLS, PATCH), 1)
    place = lax.rem(line, 8)
    patch = lax.div(line, 8)
    present = line < 0
    for kind in range(2):
        for row in range(ROWS):
            low, high = bounds(kind == 1, ROWS * t + row)
            present |= (place == kind * ROWS + row) & (patch >= DUO * low) & (patch < DUO * high)
    column = COLS * lax.rem(c + place, COLS) + patch
    half = PATCH // 2
    flows = jnp.where(
        present & (lane == column),
        flow_row,
        jnp.where(present & (lane == column + half), flow_col, 0.0),
    )
    flows = jnp.sum(flows, axis=0, keepdims=True)
    message[...] = flows
    gathered[pl.ds(SLOT[(0, 0)], 1)] = flows

    copies = [
        pltpu.make_async_remote_copy(
            src_ref=message,
            dst_ref=gathered.at[pl.ds(SLOT[(d, e)], 1)],
            send_sem=flow_send,
            recv_sem=flow_recv,
            device_id=(wrap(t - d, TILES), wrap(c - e, COLS)),
            device_id_type=MESH,
        )
        for d, e in PEERS
    ]
    for copy in copies:
        copy.start()
    field[...] = jnp.zeros_like(field)
    each_send(lambda copy: copy.wait_send())
    inbox = gathered.at[pl.ds(0, len(PEERS))]
    pltpu.make_async_copy(inbox, inbox, flow_recv).wait()

    lane = lax.broadcasted_iota(jnp.int32, (24, PATCH), 1)
    in_half = lax.rem(lane, half)
    group = lax.div(in_half, COLS)
    for q in range(2 * ROWS):
        part = jnp.zeros((24, PATCH), jnp.float32)
        for e in (-1, 0, 1):
            part += jnp.where(
                group == lax.rem(c + e + q + COLS, COLS), gathered[pl.ds((e + 1) * 24, 24)], 0.0
            )
        if q:
            near = pltpu.roll(part, PATCH - COLS * q, 1)
            far = pltpu.roll(part, half - COLS * q, 1)
            part = jnp.where(in_half + COLS * q < half, near, far)
        kind, row = divmod(q, ROWS)
        for g, tiles in enumerate(GROUPS):
            field[kind, g, pl.ds(row + g, len(tiles), stride=ROWS)] = part[8 * g : 8 * g + len(tiles)]

    size = field.shape[2:]
    flow = [field[0, g] + field[1, (g + 1) % 3] for g in range(3)]
    line = lax.broadcasted_iota(jnp.int32, size, 0)
    lane = lax.broadcasted_iota(jnp.int32, size, 1)
    column = lax.rem(lane, half)
    row = lax.rem(ROWS * t - 9 + line + ROWS * TILES, ROWS * TILES)
    in_section = lax.rem(row, SEC)
    up_ok, down_ok = in_section != 0, in_section != SEC - 1
    left_ok, right_ok = column != 0, column != half - 1
    pair_ok = [lax.rem(row + g * SEC, ROWS * TILES) < PAIR_ROWS for g in range(3)]
    shift = [jnp.zeros(size, jnp.float32) for _ in range(3)]
    for _ in range(ITERS):
        error = [
            jnp.where(pair_ok[g], shift[(g + 1) % 3] - shift[g] - flow[g], 0.0) for g in range(3)
        ]
        after = []
        for g in range(3):
            m = shift[g]
            pull = jnp.where(up_ok, m - pltpu.roll(m, 1, 0), 0.0)
            pull = pull + jnp.where(down_ok, m - pltpu.roll(m, size[0] - 1, 0), 0.0)
            pull = pull + jnp.where(left_ok, m - pltpu.roll(m, 1, 1), 0.0)
            pull = pull + jnp.where(right_ok, m - pltpu.roll(m, PATCH - 1, 1), 0.0)
            after.append(m - 0.12 * (1.0 * pull - error[g] + error[(g + 2) % 3]))
        shift = after
    result = pltpu.roll(shift[0], lax.rem(PATCH - COLS * c, PATCH), 1)
    for row in range(ROWS):
        out[row, pl.ds(0, 1)] = result[9 + row : 10 + row, 0:COLS]
        out[row, pl.ds(1, 1)] = result[9 + row : 10 + row, half : half + COLS]

    pltpu.make_async_copy(inbox, inbox, flow_send).wait()


def shards(section_image, peak_offsets):
    block = section_image.shape
    places = (2 * ROWS, COLS // DUO)
    result = pl.pallas_call(
        kernel,
        out_shape=jax.ShapeDtypeStruct((ROWS, 2, COLS), jnp.float32),
        in_specs=[pl.BlockSpec(memory_space=pl.ANY)] * 2,
        out_specs=pl.BlockSpec(memory_space=pltpu.VMEM),
        scratch_shapes=[
            pltpu.VMEM(block, jnp.bfloat16),
            pltpu.VMEM((2, *block), jnp.bfloat16),
            pltpu.SMEM((2, COLS, PAIR_ROWS), jnp.int32),
            pltpu.VMEM((DUO, 3, PATCH + 2 * PAD, PATCH), jnp.float32),
            pltpu.VMEM((11, 8 * COLS, PATCH), jnp.float32),
            pltpu.VMEM((1, PATCH), jnp.float32),
            pltpu.VMEM((72, PATCH), jnp.float32),
            pltpu.VMEM((2, 3, 24, PATCH), jnp.float32),
            pltpu.SemaphoreType.DMA((2,)),
            pltpu.SemaphoreType.DMA(places),
            pltpu.SemaphoreType.DMA(places),
            pltpu.SemaphoreType.DMA,
            pltpu.SemaphoreType.DMA,
            pltpu.SemaphoreType.REGULAR((len(ROUNDS) - 1,)),
        ],
        compiler_params=pltpu.CompilerParams(collective_id=0, has_side_effects=True),
        name="flow_and_mesh",
    )(peak_offsets.transpose(0, 2, 1), section_image)
    return result.transpose(1, 0, 2)


def solution(mesh):
    return jax.shard_map(
        shards,
        mesh=mesh,
        in_specs=(P("tile", "col"), P(None, None, "col")),
        out_specs=P(None, "tile", "col"),
        check_vma=False,
    )
```

```python
import functools

import jax
import jax.numpy as jnp
from jax import lax
from jax.experimental import pallas as pl
from jax.experimental.pallas import tpu as pltpu
from jax.sharding import PartitionSpec as P

MESH = pl.DeviceIdType.MESH
PATCH = 128
ITERS = 8
TILES = 32
COLS = 8
ROWS = 3
SEC = 32
PAIR_ROWS = 64
PAD = 16
DUO = 2

SPLIT = (
    4, 4, 4, 4, 4, 4, 4, 4, 4, 4, 6, 4, 4, 4, 4, 8,
    4, 4, 4, 4, 4, 4, 4, 4, 0, 4, 4, 6, 2, 0, 8, 4,
    4, 2, 8, 6, 0, 4, 6, 8, 4, 4, 4, 4, 2, 4, 4, 4,
    4, 4, 2, 4, 4, 4, 4, 2, 4, 4, 4, 4, 4, 4, 2, 4,
)
WORDS = tuple(sum(SPLIT[8 * w + i] // DUO << 3 * i for i in range(8)) for w in range(8))

OWN = tuple(range(-3, 4))
AHEAD = tuple(range(8, 14))
BEHIND = tuple(range(-13, -7))
GROUPS = (OWN, AHEAD, BEHIND)
FAR = tuple((d, e) for d in (-3, 3) for e in (-1, 1))
PEERS = tuple(
    (d, e) for g in GROUPS for d in g for e in (-1, 0, 1) if (d, e) not in ((0, 0), *FAR)
)
SLOT = {
    (d, e): (e + 1) * 24 + 8 * g + i
    for g, offsets in enumerate(GROUPS)
    for i, d in enumerate(offsets)
    for e in (-1, 0, 1)
}

TO_UPPER = ((2, -10, 0), (0, -11, 1), (1, -11, 2))
TO_LOWER = ((0, 10, 2), (1, 11, 0), (2, 11, 1))

BULK = ((10, 0), (11, 0), (-10, 0), (-11, 0))
SIDES = ((0, 1), (0, -1))
NEXT = ((1, 0), (-1, 0))
ROUNDS = (BULK + SIDES, BULK + SIDES, BULK + SIDES + NEXT, BULK + NEXT, BULK + NEXT)


def wrap(index, count):
    return lax.rem(index + 2 * count, count)


def kernel(
    peaks, image, out, own, other, offsets, shifted, sums, message, gathered, field,
    own_sem, send_sem, recv_sem, flow_send, flow_recv, told,
):
    t = lax.axis_index("tile")
    c = lax.axis_index("col")
    duos = COLS // DUO
    width = DUO * PATCH

    own_copy = pltpu.make_async_copy(image, own, own_sem.at[0])
    own_copy.start()
    peak_copy = pltpu.make_async_copy(peaks, offsets, own_sem.at[1])
    peak_copy.start()

    def split(pair_row):
        word = jnp.int32(WORDS[0])
        for i in range(1, 8):
            word = jnp.where(lax.div(pair_row, 8) == i, jnp.int32(WORDS[i]), word)
        return lax.shift_right_logical(word, 3 * lax.rem(pair_row, 8)) & 7

    def bounds(is_lower, row):
        pair_row = jnp.clip(row - SEC if is_lower else row, 0, PAIR_ROWS - 1)
        if is_lower:
            return jnp.where(row >= SEC, split(pair_row), duos), duos
        return 0, jnp.where(row < PAIR_ROWS, split(pair_row), 0)

    def exists(d):
        return (t + d >= 0) & (t + d < TILES)

    def tell(semaphore, peers):
        count = jnp.int32(0)
        for d, e in peers:
            count += exists(d).astype(jnp.int32)

            @pl.when(exists(d))
            def _():
                pl.semaphore_signal(
                    semaphore, inc=1, device_id=(t + d, wrap(c + e, COLS)), device_id_type=MESH
                )

        pl.semaphore_wait(semaphore, count)

    for peer in FAR:
        gathered[pl.ds(SLOT[peer], 1)] = jnp.zeros((1, PATCH), jnp.float32)
    tell(pltpu.get_barrier_semaphore(), ROUNDS[0])

    def bulk(kind, row, d, row_there, duo):
        lanes = pl.ds(pl.multiple_of(duo * width, width), width)
        place = kind * ROWS + row_there
        return pltpu.make_async_remote_copy(
            src_ref=image.at[pl.ds(row * PATCH, PATCH), lanes],
            dst_ref=other.at[kind, pl.ds(row_there * PATCH, PATCH), lanes],
            send_sem=send_sem.at[place, duo],
            recv_sem=recv_sem.at[place, duo],
            device_id=(t + d, c),
            device_id_type=MESH,
        )

    def sent(kind, row):
        there = ROWS * t + row + (SEC if kind else -SEC)
        low, high = bounds(kind == 1, there)
        if kind:
            return low, jnp.where(there < SEC * 3, high, low)
        return low, jnp.where(there >= 0, high, low)

    def each_send(act):
        for up, low in zip(TO_UPPER, TO_LOWER):
            for kind, (row, d, row_there) in enumerate((up, low)):

                def step(duo, carry, kind=kind, row=row, d=d, row_there=row_there):
                    act(bulk(kind, row, d, row_there, duo))
                    return carry

                lax.fori_loop(*sent(kind, row), step, 0)

    each_send(lambda copy: copy.start())

    for i, peers in enumerate(ROUNDS[1:]):
        tell(told.at[i], peers)

    own_copy.wait()
    peak_copy.wait()

    def one_pair(kind, row, duo, k):
        patch = duo * DUO + k
        place = kind * ROWS + row
        rows = pl.ds(row * PATCH, PATCH)
        lanes = pl.ds(pl.multiple_of(duo * width, width) + k * PATCH, PATCH)
        pair_row = ROWS * t + row - kind * SEC
        py = offsets[0, patch, pair_row]
        px = offsets[1, patch, pair_row]
        mine = own[rows, lanes].astype(jnp.float32)
        theirs = other[kind, rows, lanes].astype(jnp.float32)
        former, later = (theirs, mine) if kind else (mine, theirs)
        later = pltpu.roll(later, lax.rem(PATCH - px, PATCH), 1)
        for b in range(3):
            moved = later if b == 1 else pltpu.roll(later, 1 if b == 0 else PATCH - 1, 1)
            shifted[k, b, pl.ds(PAD, PATCH)] = moved
            shifted[k, b, pl.ds(0, PAD)] = moved[PATCH - PAD :]
            shifted[k, b, pl.ds(PAD + PATCH, PAD)] = moved[:PAD]
        at = pl.ds(patch * 8 + place, 1)
        for a in range(3):
            for b in range(3):
                product = former * shifted[k, b, pl.ds(PAD + py + a - 1, PATCH)]
                sums[3 * a + b, at] = jnp.sum(product, axis=0, keepdims=True)
        sums[9, at] = jnp.full((1, PATCH), py.astype(jnp.float32) * (1.0 / PATCH), jnp.float32)
        sums[10, at] = jnp.full((1, PATCH), px.astype(jnp.float32) * (1.0 / PATCH), jnp.float32)

    for up, low in zip(TO_UPPER, TO_LOWER):
        for kind, (_, _, row) in enumerate((up, low)):

            def step(duo, carry, kind=kind, row=row):
                lanes = pl.ds(pl.multiple_of(duo * width, width), width)
                part = other.at[kind, pl.ds(row * PATCH, PATCH), lanes]
                pltpu.make_async_copy(part, part, recv_sem.at[kind * ROWS + row, duo]).wait()
                for k in range(DUO):
                    one_pair(kind, row, duo, k)
                return carry

            lax.fori_loop(*bounds(kind == 1, ROWS * t + row), step, 0)

    total = jnp.sum(sums[...], axis=-1, keepdims=True)
    window = [total[i] * (1.0 / PATCH) for i in range(9)]
    least = functools.reduce(jnp.minimum, window)
    weight = [w - least + 0.5 for w in window]
    weight_sum = functools.reduce(jnp.add, weight)
    flow_row = total[9] + (sum(weight[6:9]) - sum(weight[0:3])) / weight_sum
    flow_col = total[10] + (sum(weight[2::3]) - sum(weight[0::3])) / weight_sum
    line = lax.broadcasted_iota(jnp.int32, (8 * COLS, PATCH), 0)
    lane = lax.broadcasted_iota(jnp.int32, (8 * COLS, PATCH), 1)
    place = lax.rem(line, 8)
    patch = lax.div(line, 8)
    present = line < 0
    for kind in range(2):
        for row in range(ROWS):
            low, high = bounds(kind == 1, ROWS * t + row)
            present |= (place == kind * ROWS + row) & (patch >= DUO * low) & (patch < DUO * high)
    column = COLS * lax.rem(c + place, COLS) + patch
    half = PATCH // 2
    flows = jnp.where(
        present & (lane == column),
        flow_row,
        jnp.where(present & (lane == column + half), flow_col, 0.0),
    )
    flows = jnp.sum(flows, axis=0, keepdims=True)
    message[...] = flows
    gathered[pl.ds(SLOT[(0, 0)], 1)] = flows

    copies = [
        pltpu.make_async_remote_copy(
            src_ref=message,
            dst_ref=gathered.at[pl.ds(SLOT[(d, e)], 1)],
            send_sem=flow_send,
            recv_sem=flow_recv,
            device_id=(wrap(t - d, TILES), wrap(c - e, COLS)),
            device_id_type=MESH,
        )
        for d, e in PEERS
    ]
    for copy in copies:
        copy.start()
    field[...] = jnp.zeros_like(field)
    each_send(lambda copy: copy.wait_send())
    inbox = gathered.at[pl.ds(0, len(PEERS))]
    pltpu.make_async_copy(inbox, inbox, flow_recv).wait()

    lane = lax.broadcasted_iota(jnp.int32, (24, PATCH), 1)
    in_half = lax.rem(lane, half)
    group = lax.div(in_half, COLS)
    for q in range(2 * ROWS):
        part = jnp.zeros((24, PATCH), jnp.float32)
        for e in (-1, 0, 1):
            part += jnp.where(
                group == lax.rem(c + e + q + COLS, COLS), gathered[pl.ds((e + 1) * 24, 24)], 0.0
            )
        if q:
            near = pltpu.roll(part, PATCH - COLS * q, 1)
            far = pltpu.roll(part, half - COLS * q, 1)
            part = jnp.where(in_half + COLS * q < half, near, far)
        kind, row = divmod(q, ROWS)
        for g, tiles in enumerate(GROUPS):
            field[kind, g, pl.ds(row + g, len(tiles), stride=ROWS)] = part[8 * g : 8 * g + len(tiles)]

    size = field.shape[2:]
    flow = [field[0, g] + field[1, (g + 1) % 3] for g in range(3)]
    line = lax.broadcasted_iota(jnp.int32, size, 0)
    lane = lax.broadcasted_iota(jnp.int32, size, 1)
    column = lax.rem(lane, half)
    row = lax.rem(ROWS * t - 9 + line + ROWS * TILES, ROWS * TILES)
    in_section = lax.rem(row, SEC)
    up_ok, down_ok = in_section != 0, in_section != SEC - 1
    left_ok, right_ok = column != 0, column != half - 1
    pair_ok = [lax.rem(row + g * SEC, ROWS * TILES) < PAIR_ROWS for g in range(3)]
    shift = [jnp.zeros(size, jnp.float32) for _ in range(3)]
    for _ in range(ITERS):
        error = [
            jnp.where(pair_ok[g], shift[(g + 1) % 3] - shift[g] - flow[g], 0.0) for g in range(3)
        ]
        after = []
        for g in range(3):
            m = shift[g]
            pull = jnp.where(up_ok, m - pltpu.roll(m, 1, 0), 0.0)
            pull = pull + jnp.where(down_ok, m - pltpu.roll(m, size[0] - 1, 0), 0.0)
            pull = pull + jnp.where(left_ok, m - pltpu.roll(m, 1, 1), 0.0)
            pull = pull + jnp.where(right_ok, m - pltpu.roll(m, PATCH - 1, 1), 0.0)
            after.append(m - 0.12 * (1.0 * pull - error[g] + error[(g + 2) % 3]))
        shift = after
    result = pltpu.roll(shift[0], lax.rem(PATCH - COLS * c, PATCH), 1)
    for row in range(ROWS):
        out[row, pl.ds(0, 1)] = result[9 + row : 10 + row, 0:COLS]
        out[row, pl.ds(1, 1)] = result[9 + row : 10 + row, half : half + COLS]

    pltpu.make_async_copy(inbox, inbox, flow_send).wait()


def shards(section_image, peak_offsets):
    block = section_image.shape
    places = (2 * ROWS, COLS // DUO)
    result = pl.pallas_call(
        kernel,
        out_shape=jax.ShapeDtypeStruct((ROWS, 2, COLS), jnp.float32),
        in_specs=[pl.BlockSpec(memory_space=pl.ANY)] * 2,
        out_specs=pl.BlockSpec(memory_space=pltpu.VMEM),
        scratch_shapes=[
            pltpu.VMEM(block, jnp.bfloat16),
            pltpu.VMEM((2, *block), jnp.bfloat16),
            pltpu.SMEM((2, COLS, PAIR_ROWS), jnp.int32),
            pltpu.VMEM((DUO, 3, PATCH + 2 * PAD, PATCH), jnp.float32),
            pltpu.VMEM((11, 8 * COLS, PATCH), jnp.float32),
            pltpu.VMEM((1, PATCH), jnp.float32),
            pltpu.VMEM((72, PATCH), jnp.float32),
            pltpu.VMEM((2, 3, 24, PATCH), jnp.float32),
            pltpu.SemaphoreType.DMA((2,)),
            pltpu.SemaphoreType.DMA(places),
            pltpu.SemaphoreType.DMA(places),
            pltpu.SemaphoreType.DMA,
            pltpu.SemaphoreType.DMA,
            pltpu.SemaphoreType.REGULAR((len(ROUNDS) - 1,)),
        ],
        compiler_params=pltpu.CompilerParams(collective_id=0, has_side_effects=True),
        name="flow_and_mesh",
    )(peak_offsets.transpose(0, 2, 1), section_image)
    return result.transpose(1, 0, 2)


def solution(mesh):
    return jax.shard_map(
        shards,
        mesh=mesh,
        in_specs=(P("tile", "col"), P(None, None, "col")),
        out_specs=P(None, "tile", "col"),
        check_vma=False,
    )
```
